32 devices in a mesh: grp: 2 (over x), seq: 16 (over z, y, core).
Axes of the slice: x: 2, y: 2, z: 4, core: 2. Of those that a mesh axis runs over, the one named last changes fastest.
Arguments:
- events: bfloat16 [24576, 1024], P(('grp', 'seq')), parts along dimension 0, may hold values from -6 to 6
- w_query: bfloat16 [1024, 1024], replicated, may hold values from -0.1875 to 0.1875
- w_key: bfloat16 [1024, 1024], replicated, may hold values from -0.1875 to 0.1875
- w_value: bfloat16 [1024, 1024], replicated, may hold values from -0.1875 to 0.1875
- w_output: bfloat16 [1024, 1024], replicated, may hold values from -0.1875 to 0.1875
- expert_in: bfloat16 [1024, 16384], P(None, 'seq'), may hold values from -0.1875 to 0.1875
- expert_out: bfloat16 [16384, 256], P('seq'), may hold values from -0.1875 to 0.1875
- gate_weight: bfloat16 [1024, 32], replicated, may hold values from -0.1875 to 0.1875
- label_rows: int32 [1024], P(('grp', 'seq')), parts along dimension 0, may hold values from 0 to 767
- label_experts: int32 [1024, 2], P(('grp', 'seq')), parts along dimension 0, may hold values from 0 to 15, all different within a row; in each aligned block of 32 rows (0 to 31, 32 to 63, ...) at most 8 rows name the same one
- label_tasks: int32 [1024], P(('grp', 'seq')), parts along dimension 0, may hold values from 0 to 1
Outputs:
- hidden: bfloat16 [24576, 1024], P(('grp', 'seq')), parts along dimension 0
- scores: float32 [1024, 256], P(('grp', 'seq')), parts along dimension 0
The draws below stay inside these ranges and needn't reach their ends.
There are 2 independent parts, one for each index of `grp`. The reference program is written for one: setup_inputs(seed, part) draws one part's arguments, and reference() takes and returns one part's arrays. A program takes and returns all parts, laid end to end along the dimension named above; an argument that names none is the same for every part. Nothing has to cross between parts.
Inputs may be any that keep to these rules, and one draw needn't show every extreme that they name: `label_experts`: each row names two different experts; within the 32 rows of one device (aligned blocks) no expert is named by more than 8 rows, and in every draw some expert is named by exactly 8 rows of some device.
All inputs are finite; a program needn't handle non-finite values.
Results may differ from the reference program's by a relative error of at most 0.012.
Values may be sent and summed in bfloat16 or wider, within the bound.
A program may use at most 128 MiB of HBM per device.

```python
import math
import jax
import jax.numpy as jnp
import numpy as np
from jax import lax

D = 1024
HEADS = 8
EXPERTS = 16
HIDDEN_SIZE = 1024
OUT = 256
TASKS = 2
CAP = 8
TOK_DEV = 768
L_DEV = 32
TOKENS = 12288
LABELS = 512


def with_ends(drawn, rng, low, high):
    longest = drawn.shape.index(max(drawn.shape))
    spots = []
    for shift in (0, 1):
        where = [jax.random.randint(jax.random.fold_in(rng, axis), (), 0, length) for axis, length in enumerate(drawn.shape)]
        where[longest] = (where[longest] + shift) % drawn.shape[longest]
        spots.append(tuple(where))
    return drawn.at[spots[0]].set(low).at[spots[1]].set(high)


def block_scale(own_key, dims, pieces, least, top_value):
    gain = 1.0
    for position, blocks in pieces:
        draws = jax.random.uniform(jax.random.fold_in(jax.random.fold_in(own_key, 6), position), (blocks,), jnp.float32, least / len(pieces), top_value / len(pieces))
        gain = gain * jnp.repeat(jnp.exp(draws), dims[position] // blocks).reshape((-1,) + (1,) * (len(dims) - 1 - position))
    return gain


def assign_block(rng, own, number, rows, number_of, top, most, lean):
    order = jax.random.permutation(rng, number_of)
    packed, ordinary = shares(number_of, rows * top, most, lean, True), shares(number_of, rows * top, most, lean, False)
    places = jnp.arange(number_of)

    def named(lengths, turn):
        used = int((lengths > 0).sum())
        fixed = max(1, used // 4)
        shifted = fixed + (places - fixed + turn * (used - fixed)) % max(1, number_of - fixed)
        return jnp.zeros((number_of,), jnp.int32).at[order[jnp.where(places < fixed, places, shifted)]].set(jnp.asarray(lengths, jnp.int32))

    lengths = jnp.where(number % 4 == 0, named(packed, number // 4), named(ordinary, number - number // 4 - 1))
    mixed = jax.random.permutation(jax.random.fold_in(own, 3), number_of)
    donor, receiver = mixed[0:number_of // 2 * 2:2], mixed[1:number_of // 2 * 2:2]
    slack = jnp.minimum(lengths[donor] - 1, most - lengths[receiver]) // 2
    slack = jnp.where((donor == order[0]) | (receiver == order[0]) | (lengths[receiver] == 0), 0, jnp.maximum(slack, 0))
    shifted = jax.random.randint(jax.random.fold_in(own, 4), (number_of // 2,), 0, 1 << 20) % (slack + 1)
    lengths = lengths.at[donor].add(-shifted).at[receiver].add(shifted)
    items = jnp.searchsorted(jnp.cumsum(lengths), jnp.arange(rows * top), side="right").astype(jnp.int32)
    grid = items.reshape(top, rows).T
    grid = grid[jax.random.permutation(jax.random.fold_in(own, 1), rows)]
    turn = jax.random.randint(jax.random.fold_in(own, 2), (rows, 1), 0, top)
    return jnp.take_along_axis(grid, (jnp.arange(top)[None, :] + turn) % top, axis=1)


def shares(amount, total, limit, lean, full):
    loads = [(1 << 20) // math.isqrt(rank ** lean) + 1 for rank in range(1, amount + 1)]
    largest = limit if full else min(limit, max(-(-total // amount), total * loads[0] // sum(loads)))
    least = 1 if total - largest >= amount - 1 else 0
    holding, rest = [largest] + [least] * (amount - 1), total - largest - least * (amount - 1)
    while rest > 0:
        free = [i for i in range(1, amount) if holding[i] < largest] or [i for i in range(1, amount) if holding[i] < limit]
        whole, remaining = sum([loads[i] for i in free]), rest
        for i in free:
            more = min(limit - holding[i], max(1, remaining * loads[i] // whole), rest)
            holding[i] = holding[i] + more
            rest = rest - more
    return np.array(holding)


def bell_draw(stream_key, extent, spread, reach, pieces=(), kind=jnp.bfloat16):
    gain = block_scale(stream_key, extent, pieces, -0.22, 0.18) if pieces else 1.0
    values = jax.random.normal(stream_key, extent, jnp.float32) * spread * gain
    return jnp.minimum(jnp.maximum(values, -reach), reach).astype(kind)


def setup_inputs(seed: int = 0, part: int = 0) -> dict:
    arg_keys = jax.random.split(jax.random.key(seed), 12)
    part_splits = jax.random.split(jax.random.fold_in(arg_keys[11], part), 12)
    events = bell_draw(part_splits[0], (TOKENS, D), 1.0, 6.0, ((0, 16),))
    w_query = bell_draw(arg_keys[1], (D, D), D ** -0.5, 0.1875)
    w_key = bell_draw(arg_keys[2], (D, D), D ** -0.5, 0.1875)
    w_value = bell_draw(arg_keys[3], (D, D), D ** -0.5, 0.1875)
    w_output = bell_draw(arg_keys[4], (D, D), D ** -0.5, 0.1875)
    expert_in = bell_draw(arg_keys[5], (D, EXPERTS * HIDDEN_SIZE), D ** -0.5, 0.1875, ((1, 16),))
    expert_out = bell_draw(arg_keys[6], (EXPERTS * HIDDEN_SIZE, OUT), HIDDEN_SIZE ** -0.5, 0.1875, ((0, 16),))
    gate_weight = bell_draw(arg_keys[7], (D, TASKS * EXPERTS), D ** -0.5, 0.1875)
    label_rows = with_ends(jax.random.randint(part_splits[8], (LABELS,), 0, TOK_DEV), jax.random.fold_in(part_splits[8], 1), 0, TOK_DEV - 1).astype(jnp.int32)
    label_experts_keys = jax.random.split(jax.random.fold_in(part_splits[9], 1), LABELS // L_DEV)
    label_experts_turns = jax.random.permutation(jax.random.fold_in(part_splits[9], 3), LABELS // L_DEV)
    label_experts = jax.vmap(lambda own, number: assign_block(jax.random.fold_in(part_splits[9], 2), own, number, L_DEV, EXPERTS, 2, CAP, 1))(label_experts_keys, label_experts_turns).reshape((LABELS, 2))
    label_tasks = with_ends(jax.random.randint(part_splits[10], (LABELS,), 0, TASKS), jax.random.fold_in(part_splits[10], 1), 0, TASKS - 1).astype(jnp.int32)
    return {"events": events, "w_query": w_query, "w_key": w_key, "w_value": w_value, "w_output": w_output, "expert_in": expert_in, "expert_out": expert_out, "gate_weight": gate_weight, "label_rows": label_rows, "label_experts": label_experts, "label_tasks": label_tasks}


def reference(events, w_query, w_key, w_value, w_output, expert_in, expert_out, gate_weight, label_rows, label_experts, label_tasks):
    head_dim = D // HEADS
    blocks = TOKENS // TOK_DEV
    query = jnp.dot(events, w_query, preferred_element_type=jnp.float32).astype(jnp.bfloat16)
    keys = jnp.dot(events, w_key, preferred_element_type=jnp.float32).astype(jnp.bfloat16)
    values = jnp.dot(events, w_value, preferred_element_type=jnp.float32).astype(jnp.bfloat16)
    query_b = query.reshape(blocks, TOK_DEV, HEADS, head_dim)
    keys_b = keys.reshape(blocks, TOK_DEV, HEADS, head_dim)
    values_b = values.reshape(blocks, TOK_DEV, HEADS, head_dim)
    local_index = jnp.arange(TOK_DEV, dtype=jnp.int32)
    causal = local_index[None, :] <= local_index[:, None]

    def advance(state, inputs):
        block_q, block_k, block_v, block_id = inputs
        prefix = lax.optimization_barrier(state.astype(jnp.bfloat16)).astype(jnp.float32)
        query_f = block_q.astype(jnp.float32)
        keys_f = block_k.astype(jnp.float32)
        values_f = block_v.astype(jnp.float32)
        weight = jnp.einsum('thd,shd->hts', query_f, keys_f)
        weight = jnp.where(causal[None], weight, 0.0)
        weight = lax.optimization_barrier(weight.astype(jnp.bfloat16)).astype(jnp.float32)
        within = jnp.einsum('hts,shd->thd', weight, values_f)
        earlier = jnp.einsum('thd,hde->the', query_f, prefix)
        places = block_id * TOK_DEV + local_index
        factor = lax.rsqrt((places + 1).astype(jnp.float32) * head_dim)
        result = ((within + earlier) * factor[:, None, None]).astype(jnp.bfloat16)
        state = state + jnp.einsum('shd,she->hde', keys_f, values_f)
        return (state, result)
    start = jnp.zeros((HEADS, head_dim, head_dim), jnp.float32)
    block_ids = jnp.arange(blocks, dtype=jnp.int32)
    final_state, attended = lax.scan(advance, start, (query_b, keys_b, values_b, block_ids))
    attended = attended.reshape(TOKENS, D)
    hidden = (events.astype(jnp.float32) + jnp.dot(attended, w_output, preferred_element_type=jnp.float32)).astype(jnp.bfloat16)
    owners = jnp.arange(LABELS, dtype=jnp.int32) // L_DEV
    picked = hidden[owners * TOK_DEV + label_rows]
    logits = jnp.dot(picked, gate_weight, preferred_element_type=jnp.float32)
    columns = label_tasks[:, None] * EXPERTS + label_experts
    gates = jax.nn.sigmoid(jnp.take_along_axis(logits, columns, axis=1))
    first_layers = expert_in.reshape(D, EXPERTS, HIDDEN_SIZE).transpose(1, 0, 2)
    second_layers = expert_out.reshape(EXPERTS, HIDDEN_SIZE, OUT)

    def one_expert(total, inputs):
        weight_in, weight_out, number = inputs
        inner = jax.nn.relu(jnp.dot(picked, weight_in, preferred_element_type=jnp.float32)).astype(jnp.bfloat16)
        output = jnp.dot(inner, weight_out, preferred_element_type=jnp.float32)
        share = lax.optimization_barrier(jnp.sum(jnp.where(label_experts == number, gates, 0.0), axis=1))
        return (total + share[:, None] * output, None)
    numbers = jnp.arange(EXPERTS, dtype=jnp.int32)
    scores, unused = lax.scan(one_expert, jnp.zeros((LABELS, OUT), jnp.float32), (first_layers, second_layers, numbers))
    return (hidden, scores)
```

```python
import functools

import jax
import jax.numpy as jnp
from jax import lax
from jax.experimental import pallas as pl
from jax.experimental.pallas import tpu as pltpu
from jax.sharding import PartitionSpec as P

HEADS = 8
EXPERTS = 16
CAP = 8
TILE = 256
MESH = pl.DeviceIdType.MESH
F32 = jnp.float32
BF16 = jnp.bfloat16


def dot(a, b):
    return jnp.dot(a, b, preferred_element_type=F32)


def dot_t(a, b):
    return lax.dot_general(a, b, (((1,), (1,)), ((), ())), preferred_element_type=F32)


def t_dot(a, b):
    return lax.dot_general(a, b, (((0,), (0,)), ((), ())), preferred_element_type=F32)


def loop(count, body):
    def step(i, carry):
        body(i)
        return carry

    lax.fori_loop(0, count, step, 0)


def kernel(
    n,
    lab_ref,
    gate_ref,
    ev_hbm,
    wq_hbm,
    wk_hbm,
    wv_hbm,
    wo_hbm,
    win_hbm,
    wout_hbm,
    hid_hbm,
    scores_ref,
    ev,
    wq,
    wk,
    wv,
    wo,
    win,
    wout,
    q_s,
    k_s,
    v_s,
    cum_s,
    within_s,
    att_s,
    hid_s,
    send1,
    recv1,
    pre2,
    pre_r,
    qp_s,
    wp_s,
    attp_s,
    pk_s,
    disp_s,
    arr_r,
    inner_s,
    back_s,
    back_r,
    load_sem,
    kv_sem,
    q_sem,
    o_sem,
    out_sem,
    ss1,
    rs1,
    ss2,
    rs2,
    ss3,
    rs3,
    ss4,
    rs4,
):
    me = lax.axis_index("seq")
    tok, width = ev.shape
    head = width // HEADS
    tiles = width // TILE
    blocks = tok // TILE
    labels = lab_ref.shape[0]
    copies = n // EXPERTS
    part = width // n
    per_head = head // part
    per_tile = n // tiles
    own = lax.rem(me, tiles) * per_tile + me // tiles
    slots = EXPERTS * CAP

    def cols_of(c):
        return pl.ds(pl.multiple_of(c * TILE, TILE), TILE)

    def head_of(h):
        return pl.ds(pl.multiple_of(h * head, head), head)

    def tile_copy(src, dst, sem, c):
        return pltpu.make_async_copy(src.at[:, cols_of(c)], dst.at[:, cols_of(c)], sem)

    def remote(src, dst, send, recv, where):
        return pltpu.make_async_remote_copy(
            src_ref=src,
            dst_ref=dst,
            send_sem=send,
            recv_sem=recv,
            device_id={"seq": where},
            device_id_type=MESH,
        )

    barrier = pltpu.get_barrier_semaphore()

    def greet(o):
        peer = lax.rem(me + o + 1, n)
        pl.semaphore_signal(barrier, inc=1, device_id={"seq": peer}, device_id_type=MESH)

    loop(n - 1, greet)

    ev_copy = pltpu.make_async_copy(ev_hbm, ev, load_sem.at[0])
    ev_copy.start()
    for c in range(tiles):
        tile_copy(wk_hbm, wk, kv_sem.at[0, c], c).start()
        tile_copy(wv_hbm, wv, kv_sem.at[1, c], c).start()
    for c in range(tiles):
        tile_copy(wq_hbm, wq, q_sem.at[c], c).start()
    wo_copy = pltpu.make_async_copy(wo_hbm, wo, load_sem.at[1])
    win_copy = pltpu.make_async_copy(win_hbm, win, load_sem.at[2])
    wout_copy = pltpu.make_async_copy(wout_hbm, wout, load_sem.at[3])
    wo_copy.start()
    win_copy.start()
    wout_copy.start()
    ev_copy.wait()

    def keys_values(c):
        cols = cols_of(c)
        tile_copy(wk_hbm, wk, kv_sem.at[0, c], c).wait()
        k_s[:, cols] = dot(ev[...], wk[:, cols]).astype(BF16)
        tile_copy(wv_hbm, wv, kv_sem.at[1, c], c).wait()
        v_s[:, cols] = dot(ev[...], wv[:, cols]).astype(BF16)
        for hh in range(TILE // head):
            h = c * (TILE // head) + hh
            hc = head_of(h)
            total = None
            for i in range(blocks):
                rows = pl.ds(i * TILE, TILE)
                state = t_dot(k_s[rows, hc], v_s[rows, hc])
                total = state if total is None else total + state
                if i < blocks - 1:
                    cum_s[i, hc, :] = total
            sent = total.astype(BF16)
            for u in range(per_head):
                send1[h * per_head + u] = sent[u * part : (u + 1) * part]

        @pl.when(c == 0)
        def _():
            pl.semaphore_wait(barrier, n - 1)

        def send(u):
            owner = u * tiles + c

            @pl.when(owner != me)
            def _():
                remote(
                    send1.at[c * per_tile + u],
                    recv1.at[me],
                    ss1.at[owner],
                    rs1.at[me],
                    owner,
                ).start()

        loop(per_tile, send)

    loop(tiles, keys_values)

    def queries(c):
        cols = cols_of(c)
        tile_copy(wq_hbm, wq, q_sem.at[c], c).wait()
        q_s[:, cols] = dot(ev[...], wq[:, cols]).astype(BF16)

    loop(tiles, queries)

    recv1[me] = send1[own]

    def await1(s):
        @pl.when(s != me)
        def _():
            remote(send1.at[0], recv1.at[s], ss1.at[s], rs1.at[s], s).wait_recv()

    loop(n, await1)

    def scan(s, acc):
        pre2[s] = acc.astype(BF16)
        return acc + recv1[s].astype(F32)

    lax.fori_loop(0, n, scan, jnp.zeros((part, recv1.shape[2]), F32))
    pre_r[own] = pre2[me]

    def send2(o):
        peer = lax.rem(me + o + 1, n)
        remote(pre2.at[peer], pre_r.at[own], ss2.at[peer], rs2.at[me], peer).start()

    loop(n - 1, send2)

    tri = lax.broadcasted_iota(jnp.int32, (TILE, TILE), 1) <= lax.broadcasted_iota(
        jnp.int32, (TILE, TILE), 0
    )

    def within(h):
        hc = head_of(h)
        for i in range(blocks):
            rows = pl.ds(i * TILE, TILE)
            w = jnp.where(tri, dot_t(q_s[rows, hc], k_s[rows, hc]), 0.0).astype(BF16)
            within_s[rows, hc] = dot(w, v_s[rows, hc])

    loop(HEADS, within)

    lab = lab_ref[...]
    row = lab[:, 0:1]
    first, second, task = lab[:, 1:2], lab[:, 2:3], lab[:, 3:4]
    places = lax.broadcasted_iota(jnp.int32, (labels, tok), 1)
    pick = jnp.where(places == row, 1.0, 0.0).astype(BF16)
    seen = places <= row
    qp_s[...] = dot(pick, q_s[...]).astype(BF16)

    def within_picked(h):
        hc = head_of(h)
        w = jnp.where(seen, dot_t(qp_s[:, hc], k_s[:, hc]), 0.0).astype(BF16)
        wp_s[:, hc] = dot(w, v_s[:, hc])

    loop(HEADS, within_picked)
    slot = lax.broadcasted_iota(jnp.int32, (labels, slots), 1)
    slot_expert, slot_rank = slot // CAP, slot % CAP
    hit0, hit1 = slot_expert == first, slot_expert == second
    named = jnp.where(hit0 | hit1, 1.0, 0.0).astype(BF16)
    lower = jnp.where(
        lax.broadcasted_iota(jnp.int32, (labels, labels), 1)
        < lax.broadcasted_iota(jnp.int32, (labels, labels), 0),
        1.0,
        0.0,
    ).astype(BF16)
    rank = dot(lower, named)
    at_rank = rank == slot_rank.astype(F32)
    sel0, sel1 = hit0 & at_rank, hit1 & at_rank
    selector = jnp.where(sel0 | sel1, 1.0, 0.0).astype(BF16)
    scale_p = lax.rsqrt((me * tok + row + 1).astype(F32) * head)

    def await2(s):
        @pl.when(s != me)
        def _():
            spot = lax.rem(s, tiles) * per_tile + s // tiles
            remote(pre2.at[s], pre_r.at[spot], ss2.at[s], rs2.at[s], s).wait_recv()

    loop(n, await2)

    def prefix_of(h):
        spots = pl.ds(h * per_head, per_head)
        return pre_r[spots].reshape(head, head)

    def attended_picked(h):
        hc = head_of(h)
        earlier = dot(qp_s[:, hc], prefix_of(h))
        attp_s[:, hc] = ((wp_s[:, hc] + earlier) * scale_p).astype(BF16)

    loop(HEADS, attended_picked)
    wo_copy.wait()

    def hidden_picked(c):
        cols = cols_of(c)
        base = dot(pick, ev[:, cols])
        pk_s[:, cols] = (base + dot(attp_s[...], wo[:, cols])).astype(BF16)
        moved = t_dot(selector, pk_s[:, cols])
        disp_s[:, :, cols] = moved.reshape(EXPERTS, CAP, TILE).astype(BF16)

    loop(tiles, hidden_picked)
    arr_r[me] = disp_s[me // copies]

    def send3(o):
        peer = lax.rem(me + o + 1, n)
        remote(
            disp_s.at[peer // copies], arr_r.at[me], ss3.at[peer], rs3.at[me], peer
        ).start()

    loop(n - 1, send3)
    logits = dot(pk_s[...], gate_ref[...])
    column = lax.broadcasted_iota(jnp.int32, logits.shape, 1)

    def gate_of(expert):
        chosen = jnp.where(column == task * EXPERTS + expert, logits, 0.0)
        return jax.nn.sigmoid(jnp.sum(chosen, axis=1, keepdims=True))

    mix = jnp.where(sel0, gate_of(first), 0.0) + jnp.where(sel1, gate_of(second), 0.0)

    def attended(h):
        hc = head_of(h)
        before = prefix_of(h)
        for i in range(blocks):
            rows = pl.ds(i * TILE, TILE)
            state = before if i == 0 else (before.astype(F32) + cum_s[i - 1, hc, :]).astype(BF16)
            place = me * tok + i * TILE + lax.broadcasted_iota(jnp.int32, (TILE, head), 0)
            scale = lax.rsqrt((place + 1).astype(F32) * head)
            att_s[rows, hc] = (
                (within_s[rows, hc] + dot(q_s[rows, hc], state)) * scale
            ).astype(BF16)

    loop(HEADS, attended)

    def hidden(c):
        cols = cols_of(c)
        hid_s[:, cols] = (ev[:, cols].astype(F32) + dot(att_s[...], wo[:, cols])).astype(BF16)
        tile_copy(hid_s, hid_hbm, out_sem.at[c], c).start()

    half = tiles // 2
    loop(half, hidden)

    win_copy.wait()
    wout_copy.wait()

    def await3(s):
        @pl.when(s != me)
        def _():
            remote(disp_s.at[0], arr_r.at[s], ss3.at[s], rs3.at[s], s).wait_recv()

    loop(n, await3)
    units = win.shape[1]
    for c in range(units // TILE):
        cols = pl.ds(c * TILE, TILE)
        arrived = arr_r[...].astype(F32).reshape(n * CAP, width).astype(BF16)
        inner_s[:, cols] = jnp.maximum(dot(arrived, win[:, cols]), 0.0).astype(BF16)
    partial = dot(inner_s[...], wout[...])
    back_s[...] = partial.reshape(n, CAP, partial.shape[1]).astype(BF16)
    back_r[me] = back_s[me]

    def send4(o):
        peer = lax.rem(me + o + 1, n)
        remote(back_s.at[peer], back_r.at[me], ss4.at[peer], rs4.at[me], peer).start()

    loop(n - 1, send4)
    loop(tiles - half, lambda c: hidden(c + half))

    def await4(s):
        @pl.when(s != me)
        def _():
            remote(back_s.at[s], back_r.at[s], ss4.at[s], rs4.at[s], s).wait_recv()

    loop(n, await4)
    back = back_r[...].astype(F32)
    if copies > 1:
        back = back.reshape(EXPERTS, copies, CAP, back.shape[2]).sum(axis=1)
    totals = back.reshape(slots, back.shape[-1])
    scores_ref[...] = jnp.dot(
        mix, totals, preferred_element_type=F32, precision=lax.Precision.HIGHEST
    )

    def sent(s):
        @pl.when(s != me)
        def _():
            remote(send1.at[0], recv1.at[s], ss1.at[s], rs1.at[s], s).wait_send()
            remote(pre2.at[s], pre_r.at[s], ss2.at[s], rs2.at[s], s).wait_send()
            remote(disp_s.at[0], arr_r.at[s], ss3.at[s], rs3.at[s], s).wait_send()
            remote(back_s.at[s], back_r.at[s], ss4.at[s], rs4.at[s], s).wait_send()

    loop(n, sent)
    for c in range(tiles):
        tile_copy(hid_s, hid_hbm, out_sem.at[c], c).wait()


def shards(
    n,
    events,
    w_query,
    w_key,
    w_value,
    w_output,
    expert_in,
    expert_out,
    gate_weight,
    label_rows,
    label_experts,
    label_tasks,
):
    tok, width = events.shape
    head = width // HEADS
    labels = label_rows.shape[0]
    units, out = expert_out.shape
    part = width // n
    tiles = width // TILE
    lab = jnp.concatenate([label_rows[:, None], label_experts, label_tasks[:, None]], axis=1)
    vmem = pl.BlockSpec(memory_space=pltpu.VMEM)
    hbm = pl.BlockSpec(memory_space=pl.ANY)
    dma = pltpu.SemaphoreType.DMA
    return pl.pallas_call(
        functools.partial(kernel, n),
        out_shape=(
            jax.ShapeDtypeStruct((tok, width), BF16),
            jax.ShapeDtypeStruct((labels, out), F32),
        ),
        in_specs=[vmem, vmem] + [hbm] * 7,
        out_specs=(hbm, vmem),
        scratch_shapes=[
            pltpu.VMEM((tok, width), BF16),
            pltpu.VMEM((width, width), BF16),
            pltpu.VMEM((width, width), BF16),
            pltpu.VMEM((width, width), BF16),
            pltpu.VMEM((width, width), BF16),
            pltpu.VMEM((width, units), BF16),
            pltpu.VMEM((units, out), BF16),
            pltpu.VMEM((tok, width), BF16),
            pltpu.VMEM((tok, width), BF16),
            pltpu.VMEM((tok, width), BF16),
            pltpu.VMEM((max(tok // TILE - 1, 1), width, head), F32),
            pltpu.VMEM((tok, width), F32),
            pltpu.VMEM((tok, width), BF16),
            pltpu.VMEM((tok, width), BF16),
            pltpu.VMEM((n, part, head), BF16),
            pltpu.VMEM((n, part, head), BF16),
            pltpu.VMEM((n, part, head), BF16),
            pltpu.VMEM((n, part, head), BF16),
            pltpu.VMEM((labels, width), BF16),
            pltpu.VMEM((labels, width), F32),
            pltpu.VMEM((labels, width), BF16),
            pltpu.VMEM((labels, width), BF16),
            pltpu.VMEM((EXPERTS, CAP, width), BF16),
            pltpu.VMEM((n, CAP, width), BF16),
            pltpu.VMEM((n * CAP, units), BF16),
            pltpu.VMEM((n, CAP, out), BF16),
            pltpu.VMEM((n, CAP, out), BF16),
            dma((4,)),
            dma((2, tiles)),
            dma((tiles,)),
            dma((1,)),
            dma((tiles,)),
        ]
        + [dma((n,))] * 8,
        compiler_params=pltpu.CompilerParams(
            collective_id=0, has_side_effects=True, vmem_limit_bytes=60 << 20
        ),
    )(
        lab,
        gate_weight,
        events,
        w_query,
        w_key,
        w_value,
        w_output,
        expert_in,
        expert_out,
    )


def solution(mesh):
    placed = (
        P(("grp", "seq"), None),
        P(),
        P(),
        P(),
        P(),
        P(None, "seq"),
        P("seq", None),
        P(),
        P(("grp", "seq")),
        P(("grp", "seq"), None),
        P(("grp", "seq")),
    )
    return jax.shard_map(
        functools.partial(shards, mesh.shape["seq"]),
        mesh=mesh,
        in_specs=placed,
        out_specs=(P(("grp", "seq"), None), P(("grp", "seq"), None)),
        check_vma=False,
    )
```

```python
import functools

import jax
import jax.numpy as jnp
from jax import lax
from jax.experimental import pallas as pl
from jax.experimental.pallas import tpu as pltpu
from jax.sharding import PartitionSpec as P

HEADS = 8
EXPERTS = 16
CAP = 8
TILE = 256
MESH = pl.DeviceIdType.MESH
F32 = jnp.float32
BF16 = jnp.bfloat16


def dot(a, b):
    return jnp.dot(a, b, preferred_element_type=F32)


def dot_t(a, b):
    return lax.dot_general(a, b, (((1,), (1,)), ((), ())), preferred_element_type=F32)


def t_dot(a, b):
    return lax.dot_general(a, b, (((0,), (0,)), ((), ())), preferred_element_type=F32)


def loop(count, body):
    def step(i, carry):
        body(i)
        return carry

    lax.fori_loop(0, count, step, 0)


def kernel(
    n,
    rows_hbm,
    experts_hbm,
    tasks_hbm,
    gate_hbm,
    ev_hbm,
    wq_hbm,
    wk_hbm,
    wv_hbm,
    wo_hbm,
    win_hbm,
    wout_hbm,
    hid_s,
    scores_ref,
    rows_s,
    experts_s,
    tasks_s,
    gate_s,
    ev,
    wq,
    wk,
    wv,
    wo,
    win,
    wout,
    q_s,
    k_s,
    v_s,
    cum_s,
    within_s,
    att_s,
    send1,
    recv1,
    pre2,
    pre_r,
    qp_s,
    wp_s,
    evp_s,
    attp_s,
    pk_s,
    disp_s,
    arr_r,
    inner_s,
    back_s,
    back_r,
    load_sem,
    kv_sem,
    q_sem,
    small_sem,
    ss1,
    rs1,
    ss2,
    rs2,
    ss3,
    rs3,
    ss4,
    rs4,
):
    me = lax.axis_index("seq")
    tok, width = ev.shape
    head = width // HEADS
    tiles = width // TILE
    blocks = tok // TILE
    labels = rows_s.shape[1]
    copies = n // EXPERTS
    part = width // n
    per_head = head // part
    per_tile = n // tiles
    own = lax.rem(me, tiles) * per_tile + me // tiles
    slots = EXPERTS * CAP

    def cols_of(c):
        return pl.ds(pl.multiple_of(c * TILE, TILE), TILE)

    def head_of(h):
        return pl.ds(pl.multiple_of(h * head, head), head)

    def tile_copy(src, dst, sem, c):
        return pltpu.make_async_copy(src.at[:, cols_of(c)], dst.at[:, cols_of(c)], sem)

    def remote(src, dst, send, recv, where):
        return pltpu.make_async_remote_copy(
            src_ref=src,
            dst_ref=dst,
            send_sem=send,
            recv_sem=recv,
            device_id={"seq": where},
            device_id_type=MESH,
        )

    barrier = pltpu.get_barrier_semaphore()

    def greet(o):
        peer = lax.rem(me + o + 1, n)
        pl.semaphore_signal(barrier, inc=1, device_id={"seq": peer}, device_id_type=MESH)

    loop(n - 1, greet)

    ev_copy = pltpu.make_async_copy(ev_hbm, ev, load_sem.at[0])
    ev_copy.start()
    for c in range(tiles):
        tile_copy(wk_hbm, wk, kv_sem.at[0, c], c).start()
        tile_copy(wv_hbm, wv, kv_sem.at[1, c], c).start()
    for c in range(tiles):
        tile_copy(wq_hbm, wq, q_sem.at[c], c).start()
    wo_copy = pltpu.make_async_copy(wo_hbm, wo, load_sem.at[1])
    win_copy = pltpu.make_async_copy(win_hbm, win, load_sem.at[2])
    wout_copy = pltpu.make_async_copy(wout_hbm, wout, load_sem.at[3])
    small = [
        pltpu.make_async_copy(src, dst, small_sem.at[i])
        for i, (src, dst) in enumerate(
            (
                (rows_hbm, rows_s),
                (experts_hbm, experts_s),
                (tasks_hbm, tasks_s),
                (gate_hbm, gate_s),
            )
        )
    ]
    for copy in small:
        copy.start()
    wo_copy.start()
    win_copy.start()
    wout_copy.start()
    ev_copy.wait()

    def keys_values(c):
        cols = cols_of(c)
        tile_copy(wk_hbm, wk, kv_sem.at[0, c], c).wait()
        k_s[:, cols] = dot(ev[...], wk[:, cols]).astype(BF16)
        tile_copy(wv_hbm, wv, kv_sem.at[1, c], c).wait()
        v_s[:, cols] = dot(ev[...], wv[:, cols]).astype(BF16)
        for hh in range(TILE // head):
            h = c * (TILE // head) + hh
            hc = head_of(h)
            total = None
            for i in range(blocks):
                rows = pl.ds(i * TILE, TILE)
                state = t_dot(k_s[rows, hc], v_s[rows, hc])
                total = state if total is None else total + state
                if i < blocks - 1:
                    cum_s[i, hc, :] = total
            sent = total.astype(BF16)
            for u in range(per_head):
                send1[h * per_head + u] = sent[u * part : (u + 1) * part]

        @pl.when(c == 0)
        def _():
            pl.semaphore_wait(barrier, n - 1)

        def send(u):
            owner = u * tiles + c

            @pl.when(owner != me)
            def _():
                remote(
                    send1.at[c * per_tile + u],
                    recv1.at[me],
                    ss1.at[owner],
                    rs1.at[me],
                    owner,
                ).start()

        loop(per_tile, send)

    loop(tiles, keys_values)

    def queries(c):
        cols = cols_of(c)
        tile_copy(wq_hbm, wq, q_sem.at[c], c).wait()
        q_s[:, cols] = dot(ev[...], wq[:, cols]).astype(BF16)

    loop(tiles, queries)

    recv1[me] = send1[own]

    def await1(s):
        @pl.when(s != me)
        def _():
            remote(send1.at[0], recv1.at[s], ss1.at[s], rs1.at[s], s).wait_recv()

    loop(n, await1)

    def scan(s, acc):
        pre2[s] = acc.astype(BF16)
        return acc + recv1[s].astype(F32)

    lax.fori_loop(0, n, scan, jnp.zeros((part, recv1.shape[2]), F32))
    pre_r[own] = pre2[me]

    def send2(o):
        peer = lax.rem(me + n // 2 + o, n)

        @pl.when(peer != me)
        def _():
            remote(pre2.at[peer], pre_r.at[own], ss2.at[peer], rs2.at[me], peer).start()

    loop(n, send2)

    tri = lax.broadcasted_iota(jnp.int32, (TILE, TILE), 1) <= lax.broadcasted_iota(
        jnp.int32, (TILE, TILE), 0
    )

    def within(h):
        hc = head_of(h)
        for i in range(blocks):
            rows = pl.ds(i * TILE, TILE)
            w = jnp.where(tri, dot_t(q_s[rows, hc], k_s[rows, hc]), 0.0).astype(BF16)
            within_s[rows, hc] = dot(w, v_s[rows, hc])

    loop(HEADS, within)

    for copy in small:
        copy.wait()
    diagonal = lax.broadcasted_iota(jnp.int32, (labels, labels), 0) == lax.broadcasted_iota(
        jnp.int32, (labels, labels), 1
    )

    def column_of(line):
        return jnp.sum(jnp.where(diagonal, line, 0), axis=1, keepdims=True)

    row = column_of(rows_s[...])
    first, second = column_of(experts_s[0:1, :]), column_of(experts_s[1:2, :])
    task = column_of(tasks_s[...])
    places = lax.broadcasted_iota(jnp.int32, (labels, tok), 1)
    pick = jnp.where(places == row, 1.0, 0.0).astype(BF16)
    seen = places <= row
    qp_s[...] = dot(pick, q_s[...]).astype(BF16)

    def within_picked(h):
        hc = head_of(h)
        w = jnp.where(seen, dot_t(qp_s[:, hc], k_s[:, hc]), 0.0).astype(BF16)
        wp_s[:, hc] = dot(w, v_s[:, hc])

    loop(HEADS, within_picked)

    def events_picked(c):
        cols = cols_of(c)
        evp_s[:, cols] = dot(pick, ev[:, cols])

    loop(tiles, events_picked)
    slot = lax.broadcasted_iota(jnp.int32, (labels, slots), 1)
    slot_expert, slot_rank = slot // CAP, slot % CAP
    hit0, hit1 = slot_expert == first, slot_expert == second
    named = jnp.where(hit0 | hit1, 1.0, 0.0).astype(BF16)
    lower = jnp.where(
        lax.broadcasted_iota(jnp.int32, (labels, labels), 1)
        < lax.broadcasted_iota(jnp.int32, (labels, labels), 0),
        1.0,
        0.0,
    ).astype(BF16)
    rank = dot(lower, named)
    at_rank = rank == slot_rank.astype(F32)
    sel0, sel1 = hit0 & at_rank, hit1 & at_rank
    selector = jnp.where(sel0 | sel1, 1.0, 0.0).astype(BF16)
    scale_p = lax.rsqrt((me * tok + row + 1).astype(F32) * head)

    def await2(s):
        @pl.when(s != me)
        def _():
            spot = lax.rem(s, tiles) * per_tile + s // tiles
            remote(pre2.at[s], pre_r.at[spot], ss2.at[s], rs2.at[s], s).wait_recv()

    loop(n, await2)

    def prefix_of(h):
        spots = pl.ds(h * per_head, per_head)
        return pre_r[spots].reshape(head, head)

    def attended_picked(h):
        hc = head_of(h)
        earlier = dot(qp_s[:, hc], prefix_of(h))
        attp_s[:, hc] = ((wp_s[:, hc] + earlier) * scale_p).astype(BF16)

    loop(HEADS, attended_picked)
    wo_copy.wait()

    def hidden_picked(c):
        cols = cols_of(c)
        pk_s[:, cols] = (evp_s[:, cols] + dot(attp_s[...], wo[:, cols])).astype(BF16)
        moved = t_dot(selector, pk_s[:, cols])
        disp_s[:, :, cols] = moved.reshape(EXPERTS, CAP, TILE).astype(BF16)

    loop(tiles, hidden_picked)
    arr_r[me] = disp_s[me // copies]

    def send3(o):
        peer = lax.rem(me + n // 2 + o, n)

        @pl.when(peer != me)
        def _():
            remote(
                disp_s.at[peer // copies], arr_r.at[me], ss3.at[peer], rs3.at[me], peer
            ).start()

    loop(n, send3)
    logits = dot_t(pk_s[...], gate_s[...])
    column = lax.broadcasted_iota(jnp.int32, logits.shape, 1)

    def gate_of(expert):
        chosen = jnp.where(column == task * EXPERTS + expert, logits, 0.0)
        return jax.nn.sigmoid(jnp.sum(chosen, axis=1, keepdims=True))

    mix = jnp.where(sel0, gate_of(first), 0.0) + jnp.where(sel1, gate_of(second), 0.0)

    def attended(h):
        hc = head_of(h)
        before = prefix_of(h)
        for i in range(blocks):
            rows = pl.ds(i * TILE, TILE)
            state = before if i == 0 else (before.astype(F32) + cum_s[i - 1, hc, :]).astype(BF16)
            place = me * tok + i * TILE + lax.broadcasted_iota(jnp.int32, (TILE, head), 0)
            scale = lax.rsqrt((place + 1).astype(F32) * head)
            att_s[rows, hc] = (
                (within_s[rows, hc] + dot(q_s[rows, hc], state)) * scale
            ).astype(BF16)

    loop(HEADS, attended)

    def hidden(c):
        cols = cols_of(c)
        hid_s[:, cols] = (ev[:, cols].astype(F32) + dot(att_s[...], wo[:, cols])).astype(BF16)

    half = tiles // 2
    loop(half, hidden)

    win_copy.wait()
    wout_copy.wait()

    def await3(s):
        @pl.when(s != me)
        def _():
            remote(disp_s.at[0], arr_r.at[s], ss3.at[s], rs3.at[s], s).wait_recv()

    loop(n, await3)
    units = win.shape[1]
    for c in range(units // TILE):
        cols = pl.ds(c * TILE, TILE)
        arrived = arr_r[...].astype(F32).reshape(n * CAP, width).astype(BF16)
        inner_s[:, cols] = jnp.maximum(dot(arrived, win[:, cols]), 0.0).astype(BF16)
    partial = dot(inner_s[...], wout[...])
    back_s[...] = partial.reshape(n, CAP, partial.shape[1]).astype(BF16)
    back_r[me] = back_s[me]

    def send4(o):
        peer = lax.rem(me + n // 2 + o, n)

        @pl.when(peer != me)
        def _():
            remote(back_s.at[peer], back_r.at[me], ss4.at[peer], rs4.at[me], peer).start()

    loop(n, send4)
    loop(tiles - half, lambda c: hidden(c + half))

    def await4(s):
        @pl.when(s != me)
        def _():
            remote(back_s.at[s], back_r.at[s], ss4.at[s], rs4.at[s], s).wait_recv()

    loop(n, await4)
    back = back_r[...].astype(F32)
    if copies > 1:
        back = back.reshape(EXPERTS, copies, CAP, back.shape[2]).sum(axis=1)
    totals = back.reshape(slots, back.shape[-1])
    scores_ref[...] = jnp.dot(
        mix, totals, preferred_element_type=F32, precision=lax.Precision.HIGHEST
    )

    def sent(s):
        @pl.when(s != me)
        def _():
            remote(send1.at[0], recv1.at[s], ss1.at[s], rs1.at[s], s).wait_send()
            remote(pre2.at[s], pre_r.at[s], ss2.at[s], rs2.at[s], s).wait_send()
            remote(disp_s.at[0], arr_r.at[s], ss3.at[s], rs3.at[s], s).wait_send()
            remote(back_s.at[s], back_r.at[s], ss4.at[s], rs4.at[s], s).wait_send()

    loop(n, sent)


def shards(
    n,
    events,
    w_query,
    w_key,
    w_value,
    w_output,
    expert_in,
    expert_out,
    gate_weight,
    label_rows,
    label_experts,
    label_tasks,
):
    tok, width = events.shape
    head = width // HEADS
    labels = label_rows.shape[0]
    units, out = expert_out.shape
    part = width // n
    tiles = width // TILE
    vmem = pl.BlockSpec(memory_space=pltpu.VMEM)
    hbm = pl.BlockSpec(memory_space=pltpu.HBM)
    dma = pltpu.SemaphoreType.DMA
    return pl.pallas_call(
        functools.partial(kernel, n),
        out_shape=(
            jax.ShapeDtypeStruct((tok, width), BF16),
            jax.ShapeDtypeStruct((labels, out), F32),
        ),
        in_specs=[hbm] * 11,
        out_specs=(vmem, vmem),
        scratch_shapes=[
            pltpu.VMEM((1, labels), jnp.int32),
            pltpu.VMEM((2, labels), jnp.int32),
            pltpu.VMEM((1, labels), jnp.int32),
            pltpu.VMEM((gate_weight.shape[1], width), BF16),
            pltpu.VMEM((tok, width), BF16),
            pltpu.VMEM((width, width), BF16),
            pltpu.VMEM((width, width), BF16),
            pltpu.VMEM((width, width), BF16),
            pltpu.VMEM((width, width), BF16),
            pltpu.VMEM((width, units), BF16),
            pltpu.VMEM((units, out), BF16),
            pltpu.VMEM((tok, width), BF16),
            pltpu.VMEM((tok, width), BF16),
            pltpu.VMEM((tok, width), BF16),
            pltpu.VMEM((max(tok // TILE - 1, 1), width, head), F32),
            pltpu.VMEM((tok, width), F32),
            pltpu.VMEM((tok, width), BF16),
            pltpu.VMEM((n, part, head), BF16),
            pltpu.VMEM((n, part, head), BF16),
            pltpu.VMEM((n, part, head), BF16),
            pltpu.VMEM((n, part, head), BF16),
            pltpu.VMEM((labels, width), BF16),
            pltpu.VMEM((labels, width), F32),
            pltpu.VMEM((labels, width), F32),
            pltpu.VMEM((labels, width), BF16),
            pltpu.VMEM((labels, width), BF16),
            pltpu.VMEM((EXPERTS, CAP, width), BF16),
            pltpu.VMEM((n, CAP, width), BF16),
            pltpu.VMEM((n * CAP, units), BF16),
            pltpu.VMEM((n, CAP, out), BF16),
            pltpu.VMEM((n, CAP, out), BF16),
            dma((4,)),
            dma((2, tiles)),
            dma((tiles,)),
            dma((4,)),
        ]
        + [dma((n,))] * 8,
        compiler_params=pltpu.CompilerParams(
            collective_id=0, has_side_effects=True, vmem_limit_bytes=40 << 20
        ),
    )(
        *[
            pltpu.with_memory_space_constraint(x, pltpu.HBM)
            for x in (
                label_rows.reshape(1, labels),
                label_experts.T,
                label_tasks.reshape(1, labels),
                gate_weight.T,
                events,
                w_query,
                w_key,
                w_value,
                w_output,
                expert_in,
                expert_out,
            )
        ]
    )


def solution(mesh):
    placed = (
        P(("grp", "seq"), None),
        P(),
        P(),
        P(),
        P(),
        P(None, "seq"),
        P("seq", None),
        P(),
        P(("grp", "seq")),
        P(("grp", "seq"), None),
        P(("grp", "seq")),
    )
    return jax.shard_map(
        functools.partial(shards, mesh.shape["seq"]),
        mesh=mesh,
        in_specs=placed,
        out_specs=(P(("grp", "seq"), None), P(("grp", "seq"), None)),
        check_vma=False,
    )
```

```python
import functools

import jax
import jax.numpy as jnp
from jax import lax
from jax.experimental import pallas as pl
from jax.experimental.pallas import tpu as pltpu
from jax.sharding import PartitionSpec as P

HEADS = 8
EXPERTS = 16
CAP = 8
TILE = 256
MESH = pl.DeviceIdType.MESH
F32 = jnp.float32
BF16 = jnp.bfloat16


def dot(a, b):
    return jnp.dot(a, b, preferred_element_type=F32)


def dot_t(a, b):
    return lax.dot_general(a, b, (((1,), (1,)), ((), ())), preferred_element_type=F32)


def t_dot(a, b):
    return lax.dot_general(a, b, (((0,), (0,)), ((), ())), preferred_element_type=F32)


def loop(count, body, wide=1):
    wide = wide if count % wide == 0 else 1

    def step(i, carry):
        for j in range(wide):
            body(i * wide + j)
        return carry

    lax.fori_loop(0, count // wide, step, 0)


def kernel(
    n,
    rows_hbm,
    experts_hbm,
    tasks_hbm,
    gate_hbm,
    ev_hbm,
    wq_hbm,
    wk_hbm,
    wv_hbm,
    wo_hbm,
    win_hbm,
    wout_hbm,
    hid_s,
    scores_ref,
    rows_s,
    experts_s,
    tasks_s,
    gate_s,
    ev,
    wq,
    wk,
    wv,
    wo,
    win,
    wout,
    q_s,
    k_s,
    v_s,
    cum_s,
    within_s,
    att_s,
    send1,
    recv1,
    pre2,
    pre_r,
    qp_s,
    wp_s,
    evp_s,
    attp_s,
    pk_s,
    disp_s,
    arr_r,
    inner_s,
    back_s,
    back_r,
    load_sem,
    kv_sem,
    q_sem,
    small_sem,
    ss1,
    rs1,
    ss2,
    rs2,
    ss3,
    rs3,
    ss4,
    rs4,
):
    me = lax.axis_index("seq")
    tok, width = ev.shape
    head = width // HEADS
    tiles = width // TILE
    blocks = tok // TILE
    labels = rows_s.shape[1]
    copies = n // EXPERTS
    part = width // n
    per_head = head // part
    per_tile = n // tiles
    own = lax.rem(me, tiles) * per_tile + me // tiles
    slots = EXPERTS * CAP

    def cols_of(c):
        return pl.ds(pl.multiple_of(c * TILE, TILE), TILE)

    def head_of(h):
        return pl.ds(pl.multiple_of(h * head, head), head)

    def tile_copy(src, dst, sem, c):
        return pltpu.make_async_copy(src.at[:, cols_of(c)], dst.at[:, cols_of(c)], sem)

    def remote(src, dst, send, recv, where):
        return pltpu.make_async_remote_copy(
            src_ref=src,
            dst_ref=dst,
            send_sem=send,
            recv_sem=recv,
            device_id={"seq": where},
            device_id_type=MESH,
        )

    barrier = pltpu.get_barrier_semaphore()

    def greet(o):
        peer = lax.rem(me + o + 1, n)
        pl.semaphore_signal(barrier, inc=1, device_id={"seq": peer}, device_id_type=MESH)

    loop(n - 1, greet)

    ev_copy = pltpu.make_async_copy(ev_hbm, ev, load_sem.at[0])
    ev_copy.start()
    for c in range(tiles):
        tile_copy(wk_hbm, wk, kv_sem.at[0, c], c).start()
        tile_copy(wv_hbm, wv, kv_sem.at[1, c], c).start()
    for c in range(tiles):
        tile_copy(wq_hbm, wq, q_sem.at[c], c).start()
    wo_copy = pltpu.make_async_copy(wo_hbm, wo, load_sem.at[1])
    win_copy = pltpu.make_async_copy(win_hbm, win, load_sem.at[2])
    wout_copy = pltpu.make_async_copy(wout_hbm, wout, load_sem.at[3])
    small = [
        pltpu.make_async_copy(src, dst, small_sem.at[i])
        for i, (src, dst) in enumerate(
            (
                (rows_hbm, rows_s),
                (experts_hbm, experts_s),
                (tasks_hbm, tasks_s),
                (gate_hbm, gate_s),
            )
        )
    ]
    for copy in small:
        copy.start()
    wo_copy.start()
    win_copy.start()
    wout_copy.start()
    ev_copy.wait()

    def keys_values(c):
        cols = cols_of(c)
        tile_copy(wk_hbm, wk, kv_sem.at[0, c], c).wait()
        k_s[:, cols] = dot(ev[...], wk[:, cols]).astype(BF16)
        tile_copy(wv_hbm, wv, kv_sem.at[1, c], c).wait()
        v_s[:, cols] = dot(ev[...], wv[:, cols]).astype(BF16)
        for hh in range(TILE // head):
            h = c * (TILE // head) + hh
            hc = head_of(h)
            total = None
            for i in range(blocks):
                rows = pl.ds(i * TILE, TILE)
                state = t_dot(k_s[rows, hc], v_s[rows, hc])
                total = state if total is None else total + state
                if i < blocks - 1:
                    cum_s[i, hc, :] = total
            sent = total.astype(BF16)
            for u in range(per_head):
                send1[h * per_head + u] = sent[u * part : (u + 1) * part]

        @pl.when(c == 0)
        def _():
            pl.semaphore_wait(barrier, n - 1)

        def send(u):
            owner = u * tiles + c

            @pl.when(owner != me)
            def _():
                remote(
                    send1.at[c * per_tile + u],
                    recv1.at[me],
                    ss1.at[owner],
                    rs1.at[me],
                    owner,
                ).start()

        loop(per_tile, send)

    loop(tiles, keys_values)

    def queries(c):
        cols = cols_of(c)
        tile_copy(wq_hbm, wq, q_sem.at[c], c).wait()
        q_s[:, cols] = dot(ev[...], wq[:, cols]).astype(BF16)

    loop(tiles, queries)

    recv1[me] = send1[own]

    def await1(s):
        @pl.when(s != me)
        def _():
            remote(send1.at[0], recv1.at[s], ss1.at[s], rs1.at[s], s).wait_recv()

    loop(n, await1)

    def scan(s, acc):
        pre2[s] = acc.astype(BF16)
        return acc + recv1[s].astype(F32)

    lax.fori_loop(0, n, scan, jnp.zeros((part, recv1.shape[2]), F32))
    pre_r[own] = pre2[me]

    def send2(o):
        peer = lax.rem(me + o, n)

        @pl.when(peer != me)
        def _():
            remote(pre2.at[peer], pre_r.at[own], ss2.at[peer], rs2.at[me], peer).start()

    loop(n, send2)

    tri = lax.broadcasted_iota(jnp.int32, (TILE, TILE), 1) <= lax.broadcasted_iota(
        jnp.int32, (TILE, TILE), 0
    )

    def within(h):
        hc = head_of(h)
        for i in range(blocks):
            rows = pl.ds(i * TILE, TILE)
            w = jnp.where(tri, dot_t(q_s[rows, hc], k_s[rows, hc]), 0.0).astype(BF16)
            within_s[rows, hc] = dot(w, v_s[rows, hc])

    loop(HEADS, within, 2)

    for copy in small:
        copy.wait()
    diagonal = lax.broadcasted_iota(jnp.int32, (labels, labels), 0) == lax.broadcasted_iota(
        jnp.int32, (labels, labels), 1
    )

    def column_of(line):
        return jnp.sum(jnp.where(diagonal, line, 0), axis=1, keepdims=True)

    row = column_of(rows_s[...])
    first, second = column_of(experts_s[0:1, :]), column_of(experts_s[1:2, :])
    task = column_of(tasks_s[...])
    places = lax.broadcasted_iota(jnp.int32, (labels, tok), 1)
    pick = jnp.where(places == row, 1.0, 0.0).astype(BF16)
    seen = places <= row
    qp_s[...] = dot(pick, q_s[...]).astype(BF16)

    def within_picked(h):
        hc = head_of(h)
        w = jnp.where(seen, dot_t(qp_s[:, hc], k_s[:, hc]), 0.0).astype(BF16)
        wp_s[:, hc] = dot(w, v_s[:, hc])

    loop(HEADS, within_picked, 4)

    def events_picked(c):
        cols = cols_of(c)
        evp_s[:, cols] = dot(pick, ev[:, cols])

    loop(tiles, events_picked, 4)
    slot = lax.broadcasted_iota(jnp.int32, (labels, slots), 1)
    slot_expert, slot_rank = slot // CAP, slot % CAP
    hit0, hit1 = slot_expert == first, slot_expert == second
    named = jnp.where(hit0 | hit1, 1.0, 0.0).astype(BF16)
    lower = jnp.where(
        lax.broadcasted_iota(jnp.int32, (labels, labels), 1)
        < lax.broadcasted_iota(jnp.int32, (labels, labels), 0),
        1.0,
        0.0,
    ).astype(BF16)
    rank = dot(lower, named)
    at_rank = rank == slot_rank.astype(F32)
    sel0, sel1 = hit0 & at_rank, hit1 & at_rank
    selector = jnp.where(sel0 | sel1, 1.0, 0.0).astype(BF16)
    scale_p = lax.rsqrt((me * tok + row + 1).astype(F32) * head)

    def await2(s):
        @pl.when(s != me)
        def _():
            spot = lax.rem(s, tiles) * per_tile + s // tiles
            remote(pre2.at[s], pre_r.at[spot], ss2.at[s], rs2.at[s], s).wait_recv()

    loop(n, await2)

    def prefix_of(h):
        spots = pl.ds(h * per_head, per_head)
        return pre_r[spots].reshape(head, head)

    def attended_picked(h):
        hc = head_of(h)
        earlier = dot(qp_s[:, hc], prefix_of(h))
        attp_s[:, hc] = ((wp_s[:, hc] + earlier) * scale_p).astype(BF16)

    loop(HEADS, attended_picked, 8)
    wo_copy.wait()

    def hidden_picked(c):
        cols = cols_of(c)
        pk_s[:, cols] = (evp_s[:, cols] + dot(attp_s[...], wo[:, cols])).astype(BF16)
        moved = t_dot(selector, pk_s[:, cols])
        disp_s[:, :, cols] = moved.reshape(EXPERTS, CAP, TILE).astype(BF16)

    loop(tiles, hidden_picked, 4)
    arr_r[me] = disp_s[me // copies]

    def send3(o):
        peer = lax.rem(me + o, n)

        @pl.when(peer != me)
        def _():
            remote(
                disp_s.at[peer // copies], arr_r.at[me], ss3.at[peer], rs3.at[me], peer
            ).start()

    loop(n, send3)
    logits = dot_t(pk_s[...], gate_s[...])
    column = lax.broadcasted_iota(jnp.int32, logits.shape, 1)

    def gate_of(expert):
        chosen = jnp.where(column == task * EXPERTS + expert, logits, 0.0)
        return jax.nn.sigmoid(jnp.sum(chosen, axis=1, keepdims=True))

    mix = jnp.where(sel0, gate_of(first), 0.0) + jnp.where(sel1, gate_of(second), 0.0)

    def attended(h):
        hc = head_of(h)
        before = prefix_of(h)
        for i in range(blocks):
            rows = pl.ds(i * TILE, TILE)
            state = before if i == 0 else (before.astype(F32) + cum_s[i - 1, hc, :]).astype(BF16)
            place = me * tok + i * TILE + lax.broadcasted_iota(jnp.int32, (TILE, head), 0)
            scale = lax.rsqrt((place + 1).astype(F32) * head)
            att_s[rows, hc] = (
                (within_s[rows, hc] + dot(q_s[rows, hc], state)) * scale
            ).astype(BF16)

    loop(HEADS, attended, 2)

    def hidden(c):
        cols = cols_of(c)
        hid_s[:, cols] = (ev[:, cols].astype(F32) + dot(att_s[...], wo[:, cols])).astype(BF16)

    half = tiles // 2
    loop(half, hidden)

    win_copy.wait()
    wout_copy.wait()

    def await3(s):
        @pl.when(s != me)
        def _():
            remote(disp_s.at[0], arr_r.at[s], ss3.at[s], rs3.at[s], s).wait_recv()

    loop(n, await3)
    units = win.shape[1]
    for c in range(units // TILE):
        cols = pl.ds(c * TILE, TILE)
        arrived = arr_r[...].astype(F32).reshape(n * CAP, width).astype(BF16)
        inner_s[:, cols] = jnp.maximum(dot(arrived, win[:, cols]), 0.0).astype(BF16)
    partial = dot(inner_s[...], wout[...])
    back_s[...] = partial.reshape(n, CAP, partial.shape[1]).astype(BF16)
    back_r[me] = back_s[me]

    def send4(o):
        peer = lax.rem(me + o, n)

        @pl.when(peer != me)
        def _():
            remote(back_s.at[peer], back_r.at[me], ss4.at[peer], rs4.at[me], peer).start()

    loop(n, send4)
    loop(tiles - half, lambda c: hidden(c + half))

    def await4(s):
        @pl.when(s != me)
        def _():
            remote(back_s.at[s], back_r.at[s], ss4.at[s], rs4.at[s], s).wait_recv()

    loop(n, await4)
    back = back_r[...].astype(F32)
    if copies > 1:
        back = back.reshape(EXPERTS, copies, CAP, back.shape[2]).sum(axis=1)
    totals = back.reshape(slots, back.shape[-1])
    scores_ref[...] = jnp.dot(
        mix, totals, preferred_element_type=F32, precision=lax.Precision.HIGHEST
    )

    def sent(s):
        @pl.when(s != me)
        def _():
            remote(send1.at[0], recv1.at[s], ss1.at[s], rs1.at[s], s).wait_send()
            remote(pre2.at[s], pre_r.at[s], ss2.at[s], rs2.at[s], s).wait_send()
            remote(disp_s.at[0], arr_r.at[s], ss3.at[s], rs3.at[s], s).wait_send()
            remote(back_s.at[s], back_r.at[s], ss4.at[s], rs4.at[s], s).wait_send()

    loop(n, sent)


def shards(
    n,
    events,
    w_query,
    w_key,
    w_value,
    w_output,
    expert_in,
    expert_out,
    gate_weight,
    label_rows,
    label_experts,
    label_tasks,
):
    tok, width = events.shape
    head = width // HEADS
    labels = label_rows.shape[0]
    units, out = expert_out.shape
    part = width // n
    tiles = width // TILE
    vmem = pl.BlockSpec(memory_space=pltpu.VMEM)
    hbm = pl.BlockSpec(memory_space=pltpu.HBM)
    dma = pltpu.SemaphoreType.DMA
    return pl.pallas_call(
        functools.partial(kernel, n),
        out_shape=(
            jax.ShapeDtypeStruct((tok, width), BF16),
            jax.ShapeDtypeStruct((labels, out), F32),
        ),
        in_specs=[hbm] * 11,
        out_specs=(vmem, vmem),
        scratch_shapes=[
            pltpu.VMEM((1, labels), jnp.int32),
            pltpu.VMEM((2, labels), jnp.int32),
            pltpu.VMEM((1, labels), jnp.int32),
            pltpu.VMEM((gate_weight.shape[1], width), BF16),
            pltpu.VMEM((tok, width), BF16),
            pltpu.VMEM((width, width), BF16),
            pltpu.VMEM((width, width), BF16),
            pltpu.VMEM((width, width), BF16),
            pltpu.VMEM((width, width), BF16),
            pltpu.VMEM((width, units), BF16),
            pltpu.VMEM((units, out), BF16),
            pltpu.VMEM((tok, width), BF16),
            pltpu.VMEM((tok, width), BF16),
            pltpu.VMEM((tok, width), BF16),
            pltpu.VMEM((max(tok // TILE - 1, 1), width, head), F32),
            pltpu.VMEM((tok, width), F32),
            pltpu.VMEM((tok, width), BF16),
            pltpu.VMEM((n, part, head), BF16),
            pltpu.VMEM((n, part, head), BF16),
            pltpu.VMEM((n, part, head), BF16),
            pltpu.VMEM((n, part, head), BF16),
            pltpu.VMEM((labels, width), BF16),
            pltpu.VMEM((labels, width), F32),
            pltpu.VMEM((labels, width), F32),
            pltpu.VMEM((labels, width), BF16),
            pltpu.VMEM((labels, width), BF16),
            pltpu.VMEM((EXPERTS, CAP, width), BF16),
            pltpu.VMEM((n, CAP, width), BF16),
            pltpu.VMEM((n * CAP, units), BF16),
            pltpu.VMEM((n, CAP, out), BF16),
            pltpu.VMEM((n, CAP, out), BF16),
            dma((4,)),
            dma((2, tiles)),
            dma((tiles,)),
            dma((4,)),
        ]
        + [dma((n,))] * 8,
        compiler_params=pltpu.CompilerParams(
            collective_id=0, has_side_effects=True, vmem_limit_bytes=40 << 20
        ),
    )(
        *[
            pltpu.with_memory_space_constraint(x, pltpu.HBM)
            for x in (
                label_rows.reshape(1, labels),
                label_experts.T,
                label_tasks.reshape(1, labels),
                gate_weight.T,
                events,
                w_query,
                w_key,
                w_value,
                w_output,
                expert_in,
                expert_out,
            )
        ]
    )


def solution(mesh):
    placed = (
        P(("grp", "seq"), None),
        P(),
        P(),
        P(),
        P(),
        P(None, "seq"),
        P("seq", None),
        P(),
        P(("grp", "seq")),
        P(("grp", "seq"), None),
        P(("grp", "seq")),
    )
    return jax.shard_map(
        functools.partial(shards, mesh.shape["seq"]),
        mesh=mesh,
        in_specs=placed,
        out_specs=(P(("grp", "seq"), None), P(("grp", "seq"), None)),
        check_vma=False,
    )
```

```python
import functools

import jax
import jax.numpy as jnp
from jax import lax
from jax.experimental import pallas as pl
from jax.experimental.pallas import tpu as pltpu
from jax.sharding import PartitionSpec as P

HEADS = 8
EXPERTS = 16
CAP = 8
TILE = 256
MESH = pl.DeviceIdType.MESH
F32 = jnp.float32
BF16 = jnp.bfloat16


def dot(a, b):
    return jnp.dot(a, b, preferred_element_type=F32)


def dot_t(a, b):
    return lax.dot_general(a, b, (((1,), (1,)), ((), ())), preferred_element_type=F32)


def t_dot(a, b):
    return lax.dot_general(a, b, (((0,), (0,)), ((), ())), preferred_element_type=F32)


def loop(count, body, wide=1):
    wide = wide if count % wide == 0 else 1

    def step(i, carry):
        for j in range(wide):
            body(i * wide + j)
        return carry

    lax.fori_loop(0, count // wide, step, 0)


def kernel(
    n,
    rows_hbm,
    experts_hbm,
    tasks_hbm,
    gate_hbm,
    ev_hbm,
    wq_hbm,
    wk_hbm,
    wv_hbm,
    wo_hbm,
    win_hbm,
    wout_hbm,
    hid_s,
    scores_ref,
    rows_s,
    experts_s,
    tasks_s,
    gate_s,
    ev,
    wq,
    wk,
    wv,
    wo,
    win,
    wout,
    q_s,
    k_s,
    v_s,
    cum_s,
    within_s,
    att_s,
    send1,
    recv1,
    pre2,
    pre_r,
    qp_s,
    wp_s,
    evp_s,
    attp_s,
    pk_s,
    disp_s,
    arr_r,
    inner_s,
    back_s,
    back_r,
    load_sem,
    kv_sem,
    q_sem,
    small_sem,
    ss1,
    rs1,
    ss2,
    rs2,
    ss3,
    rs3,
    ss4,
    rs4,
):
    me = lax.axis_index("seq")
    tok, width = ev.shape
    head = width // HEADS
    tiles = width // TILE
    blocks = tok // TILE
    labels = rows_s.shape[1]
    copies = n // EXPERTS
    part = width // n
    per_head = head // part
    per_tile = n // tiles
    own = lax.rem(me, tiles) * per_tile + me // tiles
    slots = EXPERTS * CAP

    def cols_of(c):
        return pl.ds(pl.multiple_of(c * TILE, TILE), TILE)

    def head_of(h):
        return pl.ds(pl.multiple_of(h * head, head), head)

    def tile_copy(src, dst, sem, c):
        return pltpu.make_async_copy(src.at[:, cols_of(c)], dst.at[:, cols_of(c)], sem)

    def remote(src, dst, send, recv, where):
        return pltpu.make_async_remote_copy(
            src_ref=src,
            dst_ref=dst,
            send_sem=send,
            recv_sem=recv,
            device_id={"seq": where},
            device_id_type=MESH,
        )

    barrier = pltpu.get_barrier_semaphore()

    def greet(o):
        peer = lax.rem(me + o + 1, n)
        pl.semaphore_signal(barrier, inc=1, device_id={"seq": peer}, device_id_type=MESH)

    loop(n - 1, greet)

    ev_copy = pltpu.make_async_copy(ev_hbm, ev, load_sem.at[0])
    ev_copy.start()
    for c in range(tiles):
        tile_copy(wk_hbm, wk, kv_sem.at[0, c], c).start()
        tile_copy(wv_hbm, wv, kv_sem.at[1, c], c).start()
    for c in range(tiles):
        tile_copy(wq_hbm, wq, q_sem.at[c], c).start()
    wo_copy = pltpu.make_async_copy(wo_hbm, wo, load_sem.at[1])
    win_copy = pltpu.make_async_copy(win_hbm, win, load_sem.at[2])
    wout_copy = pltpu.make_async_copy(wout_hbm, wout, load_sem.at[3])
    small = [
        pltpu.make_async_copy(src, dst, small_sem.at[i])
        for i, (src, dst) in enumerate(
            (
                (rows_hbm, rows_s),
                (experts_hbm, experts_s),
                (tasks_hbm, tasks_s),
                (gate_hbm, gate_s),
            )
        )
    ]
    for copy in small:
        copy.start()
    wo_copy.start()
    win_copy.start()
    wout_copy.start()
    ev_copy.wait()

    def keys_values(c):
        cols = cols_of(c)
        tile_copy(wk_hbm, wk, kv_sem.at[0, c], c).wait()
        k_s[:, cols] = dot(ev[...], wk[:, cols]).astype(BF16)
        tile_copy(wv_hbm, wv, kv_sem.at[1, c], c).wait()
        v_s[:, cols] = dot(ev[...], wv[:, cols]).astype(BF16)
        for hh in range(TILE // head):
            h = c * (TILE // head) + hh
            hc = head_of(h)
            total = None
            for i in range(blocks):
                rows = pl.ds(i * TILE, TILE)
                state = t_dot(k_s[rows, hc], v_s[rows, hc])
                total = state if total is None else total + state
                if i < blocks - 1:
                    cum_s[i, hc, :] = total
            sent = total.astype(BF16)
            for u in range(per_head):
                send1[h * per_head + u] = sent[u * part : (u + 1) * part]

        @pl.when(c == 0)
        def _():
            pl.semaphore_wait(barrier, n - 1)

        def send(u):
            owner = u * tiles + c

            @pl.when(owner != me)
            def _():
                remote(
                    send1.at[c * per_tile + u],
                    recv1.at[me],
                    ss1.at[owner],
                    rs1.at[me],
                    owner,
                ).start()

        loop(per_tile, send)

    loop(tiles, keys_values)

    def queries(c):
        cols = cols_of(c)
        tile_copy(wq_hbm, wq, q_sem.at[c], c).wait()
        q_s[:, cols] = dot(ev[...], wq[:, cols]).astype(BF16)

    loop(tiles, queries)

    recv1[me] = send1[own]

    def await1(s):
        @pl.when(s != me)
        def _():
            remote(send1.at[0], recv1.at[s], ss1.at[s], rs1.at[s], s).wait_recv()

    loop(n, await1)

    def scan(s, acc):
        pre2[s] = acc.astype(BF16)
        return acc + recv1[s].astype(F32)

    lax.fori_loop(0, n, scan, jnp.zeros((part, recv1.shape[2]), F32))
    pre_r[own] = pre2[me]

    def send2(o):
        peer = lax.rem(me + n // 2 + o, n)

        @pl.when(peer != me)
        def _():
            remote(pre2.at[peer], pre_r.at[own], ss2.at[peer], rs2.at[me], peer).start()

    loop(n, send2)

    tri = lax.broadcasted_iota(jnp.int32, (TILE, TILE), 1) <= lax.broadcasted_iota(
        jnp.int32, (TILE, TILE), 0
    )

    def within(h):
        hc = head_of(h)
        for i in range(blocks):
            rows = pl.ds(i * TILE, TILE)
            w = jnp.where(tri, dot_t(q_s[rows, hc], k_s[rows, hc]), 0.0).astype(BF16)
            within_s[rows, hc] = dot(w, v_s[rows, hc])

    loop(HEADS, within, 2)

    for copy in small:
        copy.wait()
    diagonal = lax.broadcasted_iota(jnp.int32, (labels, labels), 0) == lax.broadcasted_iota(
        jnp.int32, (labels, labels), 1
    )

    def column_of(line):
        return jnp.sum(jnp.where(diagonal, line, 0), axis=1, keepdims=True)

    row = column_of(rows_s[...])
    first, second = column_of(experts_s[0:1, :]), column_of(experts_s[1:2, :])
    task = column_of(tasks_s[...])
    places = lax.broadcasted_iota(jnp.int32, (labels, tok), 1)
    pick = jnp.where(places == row, 1.0, 0.0).astype(BF16)
    seen = places <= row
    qp_s[...] = dot(pick, q_s[...]).astype(BF16)

    def within_picked(h):
        hc = head_of(h)
        w = jnp.where(seen, dot_t(qp_s[:, hc], k_s[:, hc]), 0.0).astype(BF16)
        wp_s[:, hc] = dot(w, v_s[:, hc])

    loop(HEADS, within_picked, 4)

    def events_picked(c):
        cols = cols_of(c)
        evp_s[:, cols] = dot(pick, ev[:, cols])

    loop(tiles, events_picked, 4)
    slot = lax.broadcasted_iota(jnp.int32, (labels, slots), 1)
    slot_expert, slot_rank = slot // CAP, slot % CAP
    hit0, hit1 = slot_expert == first, slot_expert == second
    named = jnp.where(hit0 | hit1, 1.0, 0.0).astype(BF16)
    lower = jnp.where(
        lax.broadcasted_iota(jnp.int32, (labels, labels), 1)
        < lax.broadcasted_iota(jnp.int32, (labels, labels), 0),
        1.0,
        0.0,
    ).astype(BF16)
    rank = dot(lower, named)
    at_rank = rank == slot_rank.astype(F32)
    sel0, sel1 = hit0 & at_rank, hit1 & at_rank
    selector = jnp.where(sel0 | sel1, 1.0, 0.0).astype(BF16)
    scale_p = lax.rsqrt((me * tok + row + 1).astype(F32) * head)

    def await2(s):
        @pl.when(s != me)
        def _():
            spot = lax.rem(s, tiles) * per_tile + s // tiles
            remote(pre2.at[s], pre_r.at[spot], ss2.at[s], rs2.at[s], s).wait_recv()

    loop(n, await2)

    def prefix_of(h):
        spots = pl.ds(h * per_head, per_head)
        return pre_r[spots].reshape(head, head)

    def attended_picked(h):
        hc = head_of(h)
        earlier = dot(qp_s[:, hc], prefix_of(h))
        attp_s[:, hc] = ((wp_s[:, hc] + earlier) * scale_p).astype(BF16)

    loop(HEADS, attended_picked, 8)
    wo_copy.wait()

    def hidden_picked(c):
        cols = cols_of(c)
        pk_s[:, cols] = (evp_s[:, cols] + dot(attp_s[...], wo[:, cols])).astype(BF16)
        moved = t_dot(selector, pk_s[:, cols])
        disp_s[:, :, cols] = moved.reshape(EXPERTS, CAP, TILE).astype(BF16)

    loop(tiles, hidden_picked, 4)
    arr_r[me] = disp_s[me // copies]

    def send3(o):
        peer = lax.rem(me + n // 2 + o, n)

        @pl.when(peer != me)
        def _():
            remote(
                disp_s.at[peer // copies], arr_r.at[me], ss3.at[peer], rs3.at[me], peer
            ).start()

    loop(n, send3)
    logits = dot_t(pk_s[...], gate_s[...])
    column = lax.broadcasted_iota(jnp.int32, logits.shape, 1)

    def gate_of(expert):
        chosen = jnp.where(column == task * EXPERTS + expert, logits, 0.0)
        return jax.nn.sigmoid(jnp.sum(chosen, axis=1, keepdims=True))

    mix = jnp.where(sel0, gate_of(first), 0.0) + jnp.where(sel1, gate_of(second), 0.0)

    def attended(h):
        hc = head_of(h)
        before = prefix_of(h)
        for i in range(blocks):
            rows = pl.ds(i * TILE, TILE)
            state = before if i == 0 else (before.astype(F32) + cum_s[i - 1, hc, :]).astype(BF16)
            place = me * tok + i * TILE + lax.broadcasted_iota(jnp.int32, (TILE, head), 0)
            scale = lax.rsqrt((place + 1).astype(F32) * head)
            att_s[rows, hc] = (
                (within_s[rows, hc] + dot(q_s[rows, hc], state)) * scale
            ).astype(BF16)

    loop(HEADS, attended, 2)

    def hidden(c):
        cols = cols_of(c)
        hid_s[:, cols] = (ev[:, cols].astype(F32) + dot(att_s[...], wo[:, cols])).astype(BF16)

    half = tiles // 2
    loop(half, hidden)

    win_copy.wait()
    wout_copy.wait()

    def await3(s):
        @pl.when(s != me)
        def _():
            remote(disp_s.at[0], arr_r.at[s], ss3.at[s], rs3.at[s], s).wait_recv()

    loop(n, await3)
    units = win.shape[1]
    for c in range(units // TILE):
        cols = pl.ds(c * TILE, TILE)
        arrived = arr_r[...].astype(F32).reshape(n * CAP, width).astype(BF16)
        inner_s[:, cols] = jnp.maximum(dot(arrived, win[:, cols]), 0.0).astype(BF16)
    partial = dot(inner_s[...], wout[...])
    back_s[...] = partial.reshape(n, CAP, partial.shape[1]).astype(BF16)
    back_r[me] = back_s[me]

    def send4(o):
        peer = lax.rem(me + n // 2 + o, n)

        @pl.when(peer != me)
        def _():
            remote(back_s.at[peer], back_r.at[me], ss4.at[peer], rs4.at[me], peer).start()

    loop(n, send4)
    loop(tiles - half, lambda c: hidden(c + half))

    def await4(s):
        @pl.when(s != me)
        def _():
            remote(back_s.at[s], back_r.at[s], ss4.at[s], rs4.at[s], s).wait_recv()

    loop(n, await4)
    back = back_r[...].astype(F32)
    if copies > 1:
        back = back.reshape(EXPERTS, copies, CAP, back.shape[2]).sum(axis=1)
    totals = back.reshape(slots, back.shape[-1])
    scores_ref[...] = jnp.dot(
        mix, totals, preferred_element_type=F32, precision=lax.Precision.HIGHEST
    )

    def sent(s):
        @pl.when(s != me)
        def _():
            remote(send1.at[0], recv1.at[s], ss1.at[s], rs1.at[s], s).wait_send()
            remote(pre2.at[s], pre_r.at[s], ss2.at[s], rs2.at[s], s).wait_send()
            remote(disp_s.at[0], arr_r.at[s], ss3.at[s], rs3.at[s], s).wait_send()
            remote(back_s.at[s], back_r.at[s], ss4.at[s], rs4.at[s], s).wait_send()

    loop(n, sent)


def shards(
    n,
    events,
    w_query,
    w_key,
    w_value,
    w_output,
    expert_in,
    expert_out,
    gate_weight,
    label_rows,
    label_experts,
    label_tasks,
):
    tok, width = events.shape
    head = width // HEADS
    labels = label_rows.shape[0]
    units, out = expert_out.shape
    part = width // n
    tiles = width // TILE
    vmem = pl.BlockSpec(memory_space=pltpu.VMEM)
    hbm = pl.BlockSpec(memory_space=pltpu.HBM)
    dma = pltpu.SemaphoreType.DMA
    return pl.pallas_call(
        functools.partial(kernel, n),
        out_shape=(
            jax.ShapeDtypeStruct((tok, width), BF16),
            jax.ShapeDtypeStruct((labels, out), F32),
        ),
        in_specs=[hbm] * 11,
        out_specs=(vmem, vmem),
        scratch_shapes=[
            pltpu.VMEM((1, labels), jnp.int32),
            pltpu.VMEM((2, labels), jnp.int32),
            pltpu.VMEM((1, labels), jnp.int32),
            pltpu.VMEM((gate_weight.shape[1], width), BF16),
            pltpu.VMEM((tok, width), BF16),
            pltpu.VMEM((width, width), BF16),
            pltpu.VMEM((width, width), BF16),
            pltpu.VMEM((width, width), BF16),
            pltpu.VMEM((width, width), BF16),
            pltpu.VMEM((width, units), BF16),
            pltpu.VMEM((units, out), BF16),
            pltpu.VMEM((tok, width), BF16),
            pltpu.VMEM((tok, width), BF16),
            pltpu.VMEM((tok, width), BF16),
            pltpu.VMEM((max(tok // TILE - 1, 1), width, head), F32),
            pltpu.VMEM((tok, width), F32),
            pltpu.VMEM((tok, width), BF16),
            pltpu.VMEM((n, part, head), BF16),
            pltpu.VMEM((n, part, head), BF16),
            pltpu.VMEM((n, part, head), BF16),
            pltpu.VMEM((n, part, head), BF16),
            pltpu.VMEM((labels, width), BF16),
            pltpu.VMEM((labels, width), F32),
            pltpu.VMEM((labels, width), F32),
            pltpu.VMEM((labels, width), BF16),
            pltpu.VMEM((labels, width), BF16),
            pltpu.VMEM((EXPERTS, CAP, width), BF16),
            pltpu.VMEM((n, CAP, width), BF16),
            pltpu.VMEM((n * CAP, units), BF16),
            pltpu.VMEM((n, CAP, out), BF16),
            pltpu.VMEM((n, CAP, out), BF16),
            dma((4,)),
            dma((2, tiles)),
            dma((tiles,)),
            dma((4,)),
        ]
        + [dma((n,))] * 8,
        compiler_params=pltpu.CompilerParams(
            collective_id=0, has_side_effects=True, vmem_limit_bytes=40 << 20
        ),
    )(
        *[
            pltpu.with_memory_space_constraint(x, pltpu.HBM)
            for x in (
                label_rows.reshape(1, labels),
                label_experts.T,
                label_tasks.reshape(1, labels),
                gate_weight.T,
                events,
                w_query,
                w_key,
                w_value,
                w_output,
                expert_in,
                expert_out,
            )
        ]
    )


def solution(mesh):
    placed = (
        P(("grp", "seq"), None),
        P(),
        P(),
        P(),
        P(),
        P(None, "seq"),
        P("seq", None),
        P(),
        P(("grp", "seq")),
        P(("grp", "seq"), None),
        P(("grp", "seq")),
    )
    return jax.shard_map(
        functools.partial(shards, mesh.shape["seq"]),
        mesh=mesh,
        in_specs=placed,
        out_specs=(P(("grp", "seq"), None), P(("grp", "seq"), None)),
        check_vma=False,
    )
```
